256 devices in a mesh: stn: 16 (over z, core), seg: 16 (over x, y).
Axes of the slice: x: 4, y: 4, z: 8, core: 2. Of those that a mesh axis runs over, the one named last changes fastest.
Arguments:
- voltages: bfloat16 [128, 32, 32768], P('stn', None, 'seg'), may hold values from -91 to 91
- filter_taps: float32 [8, 32], replicated, may hold values from -0.375 to 0.375
- positions: float32 [2, 128], replicated, may hold values from -8 to 8
- beam_dirs: int32 [128], replicated, may hold values from 0 to 359
- chan_table: int32 [16], replicated, may hold values from 0 to 15, each once
Outputs:
- beam_out: bfloat16 [16, 2, 128, 32768], P('stn', None, None, 'seg')
The draws below stay inside these ranges and needn't reach their ends.
All inputs are finite; a program needn't handle non-finite values.
Results may differ from the reference program's by a relative error of at most 0.0078.
Values may be sent and summed in bfloat16 or wider, within the bound.
A program may use at most 64 MiB of HBM per device.

```python
import math
import jax
import jax.numpy as jnp
from jax import lax

S = 128
C = 16
TAPS = 8
B = 128
DIRS = 360
INTERF = 8
DMAX = 64
SNAPS = 32768
N_STN = 16


def draw_voltages(key, part):
    keys = jax.random.split(jax.random.fold_in(key, 7), 6)
    samples = SNAPS * 2 * C
    noise_part = 0.1 * jax.random.truncated_normal(keys[0], -4.0, 4.0, (S, samples), jnp.float32)
    amplitudes = jax.random.uniform(keys[3], (INTERF,), jnp.float32, 0.5, 2.0)
    station_gain = jnp.exp(jax.random.uniform(keys[5], (S, 1), jnp.float32, math.log(0.7), math.log(1.4)))
    sources = jax.random.truncated_normal(keys[1], -4.0, 4.0, (INTERF, samples + DMAX), jnp.float32)
    delays = jax.random.randint(keys[2], (INTERF, S), 0, DMAX)

    def add_source(index, summed):
        source_row = sources[index]
        shifted = jax.vmap(lambda offset: lax.dynamic_slice_in_dim(source_row, offset, samples))(delays[index])
        return summed + amplitudes[index] * shifted
    summed = lax.fori_loop(0, INTERF, add_source, noise_part) * station_gain
    return summed.reshape(S, SNAPS, 2 * C).transpose(0, 2, 1).astype(jnp.bfloat16)


def plant(drawn, rng, low, largest):
    index_at = [jax.random.randint(jax.random.fold_in(rng, axis), (), 0, length) for axis, length in enumerate(drawn.shape)]
    widest = drawn.shape.index(max(drawn.shape))
    beside = index_at[:widest] + [(index_at[widest] + 1) % drawn.shape[widest]] + index_at[widest + 1:]
    return drawn.at[tuple(index_at)].set(low).at[tuple(beside)].set(largest)


def normal_values(key, shape, width, bound, kind=jnp.bfloat16):
    return jnp.clip(width * jax.random.normal(key, shape, jnp.float32), -bound, bound).astype(kind)


def setup_inputs(seed: int = 0) -> dict:
    key_of = jax.random.split(jax.random.key(seed), 6)
    return {
        "voltages": draw_voltages(jax.random.fold_in(key_of[5], 71), 0),
        "filter_taps": normal_values(key_of[1], (TAPS, 2 * C), (TAPS * 2 * C) ** -0.5, 0.375, jnp.float32),
        "positions": jnp.clip(jax.random.uniform(key_of[2], (2, S), jnp.float32, -8.0, 8.0), -8.0, 8.0),
        "beam_dirs": plant(jax.random.randint(key_of[3], (B,), 0, DIRS), jax.random.fold_in(key_of[3], 1), 0, DIRS - 1).astype(jnp.int32),
        "chan_table": jax.random.permutation(key_of[4], C).astype(jnp.int32),
    }


loading_level = 0.1
full_turn = 2.0 * math.pi

def dft_tables(chan_table):
    frame_width = 2 * C
    phase_index = jnp.remainder(chan_table[:, None] * jnp.arange(frame_width, dtype=jnp.int32)[None, :], frame_width)
    angles = phase_index.astype(jnp.float32) * (full_turn / frame_width)
    return jnp.stack([jnp.cos(angles), -jnp.sin(angles)], axis=1)

def filter_block(station_block, filter_taps):
    snap_count = station_block.shape[2] - (TAPS - 1)
    widened = station_block.astype(jnp.float32)
    summed = jnp.zeros((station_block.shape[0], station_block.shape[1], snap_count), jnp.float32)
    for tap_index in range(TAPS):
        offset = TAPS - 1 - tap_index
        summed = summed + filter_taps[tap_index][None, :, None] * widened[:, :, offset:offset + snap_count]
    return summed

def channelize(filtered, dft_table):
    return jnp.einsum('jap,spt->jast', dft_table, filtered, precision=lax.Precision.HIGHEST).astype(jnp.bfloat16)

def halves(gram_full):
    half_size = gram_full.shape[-1] // 2
    sym_part = gram_full[..., :half_size, :half_size] + gram_full[..., half_size:, half_size:]
    skew_part = gram_full[..., half_size:, :half_size] - gram_full[..., :half_size, half_size:]
    return (sym_part, skew_part)

def assemble(sym_part, skew_part):
    upper_rows = jnp.concatenate([sym_part, -skew_part], axis=-1)
    bottom = jnp.concatenate([skew_part, sym_part], axis=-1)
    return jnp.concatenate([upper_rows, bottom], axis=-2)

def steering(positions, beam_dirs, channel):
    bearing = beam_dirs.astype(jnp.float32) * (full_turn / DIRS)
    frequency = 1.0 + channel.astype(jnp.float32) / C
    path_delay = positions[0][:, None] * jnp.cos(bearing)[None, :] + positions[1][:, None] * jnp.sin(bearing)[None, :]
    phases = full_turn * frequency * path_delay
    return jnp.concatenate([jnp.cos(phases), jnp.sin(phases)], axis=0)

def solve_weights(factor, steer):
    whitened = jax.scipy.linalg.solve_triangular(factor, steer, lower=True)
    column_power = lax.optimization_barrier(jnp.sum(whitened * whitened, axis=0))
    solved = jax.scipy.linalg.solve_triangular(factor, whitened, lower=True, trans=1)
    return (solved / jnp.sqrt(column_power)[None, :]).astype(jnp.bfloat16)

def mixing(weights):
    half_size = weights.shape[0] // 2
    swapped = jnp.concatenate([-weights[half_size:], weights[:half_size]], axis=0)
    return jnp.concatenate([weights.T, swapped.T], axis=0)

def reference(voltages, filter_taps, positions, beam_dirs, chan_table):
    dft_table = dft_tables(chan_table)
    padded = jnp.pad(voltages, ((0, 0), (0, 0), (TAPS - 1, 0)))
    station_blocks = padded.reshape(N_STN, S // N_STN, 2 * C, SNAPS + TAPS - 1)
    spectra = lax.map(lambda station_block: channelize(filter_block(station_block, filter_taps), dft_table), station_blocks)
    spectra = jnp.transpose(spectra, (1, 2, 0, 3, 4)).reshape(C, 2 * S, SNAPS)
    identity = jnp.eye(2 * S, dtype=jnp.float32)

    def one_channel(channel_item):
        stacked, channel = channel_item
        gram_full = jnp.dot(stacked.astype(jnp.float32), stacked.T.astype(jnp.float32), preferred_element_type=jnp.float32)
        sym_part, skew_part = halves(gram_full)
        covariance = assemble(sym_part, skew_part) / SNAPS + loading_level * identity
        factor = jnp.linalg.cholesky(covariance)
        weights = solve_weights(factor, steering(positions, beam_dirs, channel))
        mix_matrix = mixing(weights)
        beam_out = jnp.dot(mix_matrix.astype(jnp.float32), stacked.astype(jnp.float32), preferred_element_type=jnp.float32)
        return beam_out.astype(jnp.bfloat16).reshape(2, B, SNAPS)
    return lax.map(one_channel, (spectra, chan_table))
```

```python
import functools
import math

import jax
import jax.numpy as jnp
from jax import lax
from jax.experimental import pallas as pl
from jax.experimental.pallas import tpu as pltpu
from jax.sharding import PartitionSpec as P

C = 16
TAPS = 8
B = 128
DIRS = 360
S = 128
SEG = 16


loading_level = 0.1
full_turn = 2.0 * math.pi
HIGHEST = lax.Precision.HIGHEST
MESH = pl.DeviceIdType.MESH


def passed_along(value, axis, by):
    length = lax.axis_size(axis)
    pairs = [(i, i + by) for i in range(length) if 0 <= i + by < length]
    return lax.ppermute(value, axis, pairs)


def dft_tables(chan_table):
    frame_width = 2 * C
    phase_index = jnp.remainder(
        chan_table[:, None] * jnp.arange(frame_width, dtype=jnp.int32)[None, :], frame_width
    )
    angles = phase_index.astype(jnp.float32) * (full_turn / frame_width)
    return jnp.stack([jnp.cos(angles), -jnp.sin(angles)], axis=1)


def filter_block(station_block, filter_taps):
    snap_count = station_block.shape[2] - (TAPS - 1)
    widened = station_block.astype(jnp.float32)
    summed = jnp.zeros((station_block.shape[0], station_block.shape[1], snap_count), jnp.float32)
    for tap_index in range(TAPS):
        offset = TAPS - 1 - tap_index
        summed = (
            summed
            + filter_taps[tap_index][None, :, None] * widened[:, :, offset : offset + snap_count]
        )
    return summed


def channelize(filtered, dft_table):
    return jnp.einsum("jap,spt->jast", dft_table, filtered, precision=HIGHEST).astype(
        jnp.bfloat16
    )


def steering(positions, beam_dirs, channel):
    bearing = beam_dirs.astype(jnp.float32) * (full_turn / DIRS)
    frequency = 1.0 + channel.astype(jnp.float32) / C
    path_delay = (
        positions[0][:, None] * jnp.cos(bearing)[None, :]
        + positions[1][:, None] * jnp.sin(bearing)[None, :]
    )
    phases = full_turn * frequency * path_delay
    return jnp.concatenate([jnp.cos(phases), jnp.sin(phases)], axis=0)


def seg_sum_kernel(part_ref, sum_ref, landed, send_a, recv_a, send_b, recv_b):
    me = lax.axis_index("seg")
    barrier = pltpu.get_barrier_semaphore()
    peers = [lax.rem(me + d, SEG) for d in range(1, SEG)]
    for peer in peers:
        pl.semaphore_signal(barrier, inc=1, device_id={"seg": peer}, device_id_type=MESH)
    pl.semaphore_wait(barrier, SEG - 1)
    spread = []
    for d, peer in enumerate(peers):
        copy = pltpu.make_async_remote_copy(
            src_ref=part_ref.at[peer],
            dst_ref=landed.at[d],
            send_sem=send_a.at[d],
            recv_sem=recv_a.at[d],
            device_id={"seg": peer},
            device_id_type=MESH,
        )
        copy.start()
        spread.append(copy)
    total = part_ref[me]
    for d, copy in enumerate(spread):
        copy.wait_recv()
        total = total + landed[d]
    sum_ref[me] = total
    shared = []
    for d, peer in enumerate(peers):
        copy = pltpu.make_async_remote_copy(
            src_ref=sum_ref.at[me],
            dst_ref=sum_ref.at[me],
            send_sem=send_b.at[d],
            recv_sem=recv_b.at[d],
            device_id={"seg": peer},
            device_id_type=MESH,
        )
        copy.start()
        shared.append(copy)
    for copy in spread:
        copy.wait_send()
    for copy in shared:
        copy.wait()


def seg_sum(part):
    rows = S // SEG
    vmem = pl.BlockSpec(memory_space=pltpu.VMEM)
    return pl.pallas_call(
        seg_sum_kernel,
        out_shape=jax.ShapeDtypeStruct((SEG, rows, S), jnp.float32),
        in_specs=[vmem],
        out_specs=vmem,
        scratch_shapes=[
            pltpu.VMEM((SEG - 1, rows, S), jnp.float32),
            pltpu.SemaphoreType.DMA((SEG - 1,)),
            pltpu.SemaphoreType.DMA((SEG - 1,)),
            pltpu.SemaphoreType.DMA((SEG - 1,)),
            pltpu.SemaphoreType.DMA((SEG - 1,)),
        ],
        compiler_params=pltpu.CompilerParams(collective_id=1, has_side_effects=True),
        name="seg_sum",
    )(part.reshape(SEG, rows, S)).reshape(S, S)


def invert_hermitian(hr_ref, hi_ref):
    groups = S // 8
    lane = lax.broadcasted_iota(jnp.int32, (8, S), 1)
    row = lax.broadcasted_iota(jnp.int32, (8, S), 0)

    def trip(_, carry):
        hr = [hr_ref[pl.ds(8 * g, 8), :] for g in range(groups)]
        hi = [hi_ref[pl.ds(8 * g, 8), :] for g in range(groups)]
        pr, pi = hr[0], hi[0]
        for i in range(8):
            cr, ci = pr[:, i : i + 1], pi[:, i : i + 1]
            inv = 1.0 / pr[i : i + 1, i : i + 1]
            at = lane[0:1] == i
            rr = jnp.where(at, inv, pr[i : i + 1, :] * inv)
            ri = jnp.where(at, 0.0, pi[i : i + 1, :] * inv)
            br = jnp.where(lane == i, 0.0, pr)
            bi = jnp.where(lane == i, 0.0, pi)
            nr = br - (cr * rr - ci * ri)
            ni = bi - (cr * ri + ci * rr)
            pr = jnp.where(row == i, rr, nr)
            pi = jnp.where(row == i, ri, ni)
        for g in range(1, groups):
            ar = jnp.where(lane < 8, 0.0, hr[g])
            ai = jnp.where(lane < 8, 0.0, hi[g])
            for i in range(8):
                cr, ci = hr[g][:, i : i + 1], hi[g][:, i : i + 1]
                rr, ri = pr[i : i + 1, :], pi[i : i + 1, :]
                ar = ar - (cr * rr - ci * ri)
                ai = ai - (cr * ri + ci * rr)
            hr_ref[pl.ds(8 * (g - 1), 8), :] = pltpu.roll(ar, S - 8, 1)
            hi_ref[pl.ds(8 * (g - 1), 8), :] = pltpu.roll(ai, S - 8, 1)
        hr_ref[pl.ds(S - 8, 8), :] = pltpu.roll(pr, S - 8, 1)
        hi_ref[pl.ds(S - 8, 8), :] = pltpu.roll(pi, S - 8, 1)
        return carry

    lax.fori_loop(0, groups, trip, 0)


def beam_kernel(snap_total, packed_ref, steer_ref, stacked_ref, out_ref, hr_ref, hi_ref):
    packed = packed_ref[...]
    turned = packed.T
    row = lax.broadcasted_iota(jnp.int32, (S, S), 0)
    lane = lax.broadcasted_iota(jnp.int32, (S, S), 1)
    upper = lane > row
    diag = lane == row
    sym = jnp.where(upper, turned, packed) / snap_total
    skew = jnp.where(upper, packed, -turned) / snap_total
    hr_ref[...] = sym + jnp.where(diag, loading_level, 0.0)
    hi_ref[...] = jnp.where(diag, 0.0, skew)
    invert_hermitian(hr_ref, hi_ref)
    vr, vi = steer_ref[0:S], steer_ref[S : 2 * S]
    both = jnp.concatenate([vr, vi], axis=1)
    by_real = jnp.dot(hr_ref[...], both, precision=HIGHEST, preferred_element_type=jnp.float32)
    by_imag = jnp.dot(hi_ref[...], both, precision=HIGHEST, preferred_element_type=jnp.float32)
    wr = by_real[:, :B] - by_imag[:, B:]
    wi = by_real[:, B:] + by_imag[:, :B]
    power = jnp.sum(vr * wr + vi * wi, axis=0, keepdims=True)
    scale = 1.0 / jnp.sqrt(power)
    wr = (wr * scale).astype(jnp.bfloat16)
    wi = (wi * scale).astype(jnp.bfloat16)
    weights = jnp.concatenate([wr, wi], axis=0)
    swapped = jnp.concatenate([-wi, wr], axis=0)
    mix = jnp.concatenate([weights, swapped], axis=1).T
    width = 512

    def tile(n, carry):
        at = pl.ds(pl.multiple_of(n * width, width), width)
        res = jnp.dot(mix, stacked_ref[:, at], preferred_element_type=jnp.float32)
        out_ref[:, at] = res.astype(jnp.bfloat16)
        return carry

    lax.fori_loop(0, stacked_ref.shape[1] // width, tile, 0)


def beams(packed, steer, stacked, snap_total):
    vmem = pl.BlockSpec(memory_space=pltpu.VMEM)
    return pl.pallas_call(
        functools.partial(beam_kernel, snap_total),
        out_shape=jax.ShapeDtypeStruct((2 * B, stacked.shape[1]), jnp.bfloat16),
        in_specs=[vmem, vmem, vmem],
        out_specs=vmem,
        scratch_shapes=[pltpu.VMEM((S, S), jnp.float32), pltpu.VMEM((S, S), jnp.float32)],
        name="beams",
    )(packed, steer, stacked)


def on_device(voltages, filter_taps, positions, beam_dirs, chan_table):
    last_frames = voltages[:, :, voltages.shape[2] - (TAPS - 1) :]
    earlier = passed_along(last_frames, "seg", 1)
    extended = jnp.concatenate([earlier, voltages], axis=2)
    filtered = filter_block(extended, filter_taps)
    spectra = channelize(filtered, dft_tables(chan_table))
    turned = lax.all_to_all(spectra, "stn", split_axis=0, concat_axis=2, tiled=True)
    snap_count = turned.shape[3]
    stacked = turned.reshape(2 * S, snap_count)
    gram = jnp.einsum("at,bt->ab", stacked, stacked, preferred_element_type=jnp.float32)
    sym_part = gram[:S, :S] + gram[S:, S:]
    skew_part = gram[S:, :S] - gram[:S, S:]
    upper = jnp.arange(S)[None, :] > jnp.arange(S)[:, None]
    packed = seg_sum(jnp.where(upper, skew_part, sym_part))
    channel = lax.dynamic_index_in_dim(chan_table, lax.axis_index("stn"), keepdims=False)
    steer = steering(positions, beam_dirs, channel)
    beam_out = beams(packed, steer, stacked, float(snap_count * SEG))
    return beam_out.reshape(1, 2, B, snap_count)


def solution(mesh):
    return jax.shard_map(
        on_device,
        mesh=mesh,
        in_specs=(P("stn", None, "seg"), P(), P(), P(), P()),
        out_specs=P("stn", None, None, "seg"),
        check_vma=False,
    )
```

```python
import functools
import math

import jax
import jax.numpy as jnp
from jax import lax
from jax.experimental import pallas as pl
from jax.experimental.pallas import tpu as pltpu
from jax.sharding import PartitionSpec as P

C = 16
TAPS = 8
B = 128
DIRS = 360
S = 128
SEG = 16
STN = 16
CHUNKS = 4
PAD = 128


loading_level = 0.1
full_turn = 2.0 * math.pi
HIGHEST = lax.Precision.HIGHEST
MESH = pl.DeviceIdType.MESH


def front_kernel(
    v_ref, taps_ref, pos_ref, dirs_ref, chan_ref,
    packed_ref, steer_ref, out_ref,
    vbuf, spread, spec, land, gram, part, landed,
    vsem, osem, hsem, send_x, recv_x, send_a, recv_a, send_b, recv_b,
):
    stn, seg = lax.axis_index("stn"), lax.axis_index("seg")
    stn_peers = [lax.rem(stn + d, STN) for d in range(1, STN)]
    seg_peers = [lax.rem(seg + d, SEG) for d in range(1, SEG)]
    local = v_ref.shape[0]
    snaps = v_ref.shape[2]
    wide = snaps // CHUNKS
    frame = 2 * C

    barrier = pltpu.get_barrier_semaphore()
    for peer in stn_peers:
        pl.semaphore_signal(barrier, inc=1, device_id={"stn": peer}, device_id_type=MESH)
    for peer in seg_peers:
        pl.semaphore_signal(barrier, inc=1, device_id={"seg": peer}, device_id_type=MESH)
    fetches = []
    for c in range(CHUNKS):
        fetch = pltpu.make_async_copy(
            v_ref.at[:, :, pl.ds(c * wide, wide)],
            vbuf.at[:, :, pl.ds(PAD + c * wide, wide)],
            vsem.at[c],
        )
        fetch.start()
        fetches.append(fetch)

    row = lax.broadcasted_iota(jnp.int32, (frame, TAPS * frame), 0)
    lane = lax.broadcasted_iota(jnp.int32, (frame, TAPS * frame), 1)
    channel_of = jnp.zeros((frame, TAPS * frame), jnp.int32)
    for j in range(C):
        channel_of = jnp.where(row // 2 == j, chan_ref[j], channel_of)
    phase_index = jnp.bitwise_and(channel_of * jnp.bitwise_and(lane, frame - 1), frame - 1)
    angles = phase_index.astype(jnp.float32) * (full_turn / frame)
    table = jnp.where(row % 2 == 0, jnp.cos(angles), -jnp.sin(angles))
    taps = jnp.concatenate([taps_ref[m : m + 1, :] for m in range(TAPS)], axis=1)
    mixed = table * taps
    high = mixed.astype(jnp.bfloat16)
    low = (mixed - high.astype(jnp.float32)).astype(jnp.bfloat16)
    mixed = jnp.concatenate([high, low], axis=0)

    def channelize_chunk(c):
        def station(s, carry):
            x = vbuf[s, :, pl.ds(c * wide, wide + PAD)]
            moved = [x[:, PAD - m : PAD - m + wide] for m in range(TAPS)]
            res = jnp.dot(
                mixed, jnp.concatenate(moved, axis=0), preferred_element_type=jnp.float32
            )
            res = res[:frame] + res[frame:]
            for q in range(wide // PAD):
                spread[q, pl.ds(pl.multiple_of(s * frame, frame), frame), :] = res[
                    :, q * PAD : (q + 1) * PAD
                ]
            return carry

        lax.fori_loop(0, local, station, 0, unroll=2)
        for j in range(C):
            for a in range(2):
                for q in range(wide // PAD):
                    picked = spread[q, pl.ds(2 * j + a, local, stride=frame), :]
                    spec[c, j, a, :, q * PAD : (q + 1) * PAD] = picked.astype(jnp.bfloat16)

    def send_chunk(c):
        copies = []
        for d, peer in enumerate(stn_peers):
            copy = pltpu.make_async_remote_copy(
                src_ref=spec.at[c, peer],
                dst_ref=land.at[:, stn, :, pl.ds(c * wide, wide)],
                send_sem=send_x.at[c, d],
                recv_sem=recv_x.at[c, d],
                device_id={"stn": peer},
                device_id_type=MESH,
            )
            copy.start()
            copies.append(copy)
        land[:, stn, :, pl.ds(c * wide, wide)] = spec[c, stn]
        return copies

    order = list(range(1, CHUNKS)) + [0]
    for c in range(2):
        fetches[c].wait()
    channelize_chunk(order[0])
    pl.semaphore_wait(barrier, STN - 1 + SEG - 1)
    halo = pltpu.make_async_remote_copy(
        src_ref=v_ref.at[:, :, pl.ds(snaps - PAD, PAD)],
        dst_ref=vbuf.at[:, :, pl.ds(0, PAD)],
        send_sem=hsem.at[0],
        recv_sem=hsem.at[1],
        device_id={"seg": seg_peers[0]},
        device_id_type=MESH,
    )
    halo.start()
    sent = {order[0]: send_chunk(order[0])}
    for c in order[1:]:
        if c >= 2:
            fetches[c].wait()
        if c == 0:
            halo.wait()

            @pl.when(seg == 0)
            def _():
                vbuf[:, :, 0:PAD] = jnp.zeros((local, frame, PAD), jnp.bfloat16)

        channelize_chunk(c)
        sent[c] = send_chunk(c)

    bearing = dirs_ref[...].astype(jnp.float32) * (full_turn / DIRS)
    frequency = 1.0 + chan_ref[stn].astype(jnp.float32) / C
    east = jnp.broadcast_to(pos_ref[0:1, :], (S, S)).T
    north = jnp.broadcast_to(pos_ref[1:2, :], (S, S)).T
    phases = (full_turn * frequency) * (east * jnp.cos(bearing) + north * jnp.sin(bearing))
    steer_ref[0:S, :] = jnp.cos(phases)
    steer_ref[S : 2 * S, :] = jnp.sin(phases)

    stores = []
    for n, c in enumerate(order):
        for copy in sent[c]:
            copy.wait_recv()
        at = pl.ds(c * wide, wide)
        store = pltpu.make_async_copy(land.at[:, :, :, at], out_ref.at[:, :, :, at], osem.at[c])
        store.start()
        stores.append(store)
        block = land[:, :, :, at].reshape(2 * S, wide)
        term = lax.dot_general(
            block, block, (((1,), (1,)), ((), ())), preferred_element_type=jnp.float32
        )
        if n == 0:
            gram[...] = term
        else:
            gram[...] += term

    sym = gram[0:S, 0:S] + gram[S : 2 * S, S : 2 * S]
    skew = gram[S : 2 * S, 0:S] - gram[0:S, S : 2 * S]
    row = lax.broadcasted_iota(jnp.int32, (S, S), 0)
    lane = lax.broadcasted_iota(jnp.int32, (S, S), 1)
    part[...] = jnp.where(lane > row, skew, sym).reshape(part.shape)

    spread_out = []
    for d, peer in enumerate(seg_peers):
        copy = pltpu.make_async_remote_copy(
            src_ref=part.at[peer],
            dst_ref=landed.at[d],
            send_sem=send_a.at[d],
            recv_sem=recv_a.at[d],
            device_id={"seg": peer},
            device_id_type=MESH,
        )
        copy.start()
        spread_out.append(copy)
    total = part[seg]
    for d, copy in enumerate(spread_out):
        copy.wait_recv()
        total = total + landed[d]
    packed_ref[seg] = total
    shared = []
    for d, peer in enumerate(seg_peers):
        copy = pltpu.make_async_remote_copy(
            src_ref=packed_ref.at[seg],
            dst_ref=packed_ref.at[seg],
            send_sem=send_b.at[d],
            recv_sem=recv_b.at[d],
            device_id={"seg": peer},
            device_id_type=MESH,
        )
        copy.start()
        shared.append(copy)
    for c in order:
        for copy in sent[c]:
            copy.wait_send()
    for store in stores:
        store.wait()
    for copy in spread_out:
        copy.wait_send()
    for copy in shared:
        copy.wait()


def front(voltages, filter_taps, positions, beam_dirs, chan_table):
    local, frame, snaps = voltages.shape
    wide = snaps // CHUNKS
    rows = S // SEG
    vmem = pl.BlockSpec(memory_space=pltpu.VMEM)
    hbm = pl.BlockSpec(memory_space=pl.ANY)
    smem = pl.BlockSpec(memory_space=pltpu.SMEM)
    dma = pltpu.SemaphoreType.DMA
    return pl.pallas_call(
        front_kernel,
        out_shape=(
            jax.ShapeDtypeStruct((SEG, rows, S), jnp.float32),
            jax.ShapeDtypeStruct((2 * S, B), jnp.float32),
            jax.ShapeDtypeStruct((2, STN, local, snaps), jnp.bfloat16),
        ),
        in_specs=[hbm, vmem, vmem, vmem, smem],
        out_specs=(vmem, vmem, hbm),
        scratch_shapes=[
            pltpu.VMEM((local, frame, PAD + snaps), jnp.bfloat16),
            pltpu.VMEM((wide // PAD, local * frame, PAD), jnp.float32),
            pltpu.VMEM((CHUNKS, STN, 2, local, wide), jnp.bfloat16),
            pltpu.VMEM((2, STN, local, snaps), jnp.bfloat16),
            pltpu.VMEM((2 * S, 2 * S), jnp.float32),
            pltpu.VMEM((SEG, rows, S), jnp.float32),
            pltpu.VMEM((SEG - 1, rows, S), jnp.float32),
            dma((CHUNKS,)),
            dma((CHUNKS,)),
            dma((2,)),
            dma((CHUNKS, STN - 1)),
            dma((CHUNKS, STN - 1)),
            dma((SEG - 1,)),
            dma((SEG - 1,)),
            dma((SEG - 1,)),
            dma((SEG - 1,)),
        ],
        compiler_params=pltpu.CompilerParams(
            collective_id=1, has_side_effects=True, vmem_limit_bytes=32 * 1024 * 1024
        ),
        name="front",
    )(voltages, filter_taps, positions, beam_dirs.reshape(1, B), chan_table)


def invert_hermitian(hr_ref, hi_ref):
    groups = S // 8
    lane = lax.broadcasted_iota(jnp.int32, (8, S), 1)
    row = lax.broadcasted_iota(jnp.int32, (8, S), 0)

    def trip(_, carry):
        hr = [hr_ref[pl.ds(8 * g, 8), :] for g in range(groups)]
        hi = [hi_ref[pl.ds(8 * g, 8), :] for g in range(groups)]
        pr, pi = hr[0], hi[0]
        for i in range(8):
            cr, ci = pr[:, i : i + 1], pi[:, i : i + 1]
            inv = 1.0 / pr[i : i + 1, i : i + 1]
            at = lane[0:1] == i
            rr = jnp.where(at, inv, pr[i : i + 1, :] * inv)
            ri = jnp.where(at, 0.0, pi[i : i + 1, :] * inv)
            br = jnp.where(lane == i, 0.0, pr)
            bi = jnp.where(lane == i, 0.0, pi)
            nr = br - (cr * rr - ci * ri)
            ni = bi - (cr * ri + ci * rr)
            pr = jnp.where(row == i, rr, nr)
            pi = jnp.where(row == i, ri, ni)
        for g in range(1, groups):
            ar = jnp.where(lane < 8, 0.0, hr[g])
            ai = jnp.where(lane < 8, 0.0, hi[g])
            for i in range(8):
                cr, ci = hr[g][:, i : i + 1], hi[g][:, i : i + 1]
                rr, ri = pr[i : i + 1, :], pi[i : i + 1, :]
                ar = ar - (cr * rr - ci * ri)
                ai = ai - (cr * ri + ci * rr)
            hr_ref[pl.ds(8 * (g - 1), 8), :] = pltpu.roll(ar, S - 8, 1)
            hi_ref[pl.ds(8 * (g - 1), 8), :] = pltpu.roll(ai, S - 8, 1)
        hr_ref[pl.ds(S - 8, 8), :] = pltpu.roll(pr, S - 8, 1)
        hi_ref[pl.ds(S - 8, 8), :] = pltpu.roll(pi, S - 8, 1)
        return carry

    lax.fori_loop(0, groups, trip, 0)


def beam_kernel(snap_total, packed_ref, steer_ref, held_ref, out_ref, hr_ref, hi_ref, stacked_ref, sem):
    fetch = pltpu.make_async_copy(held_ref, stacked_ref, sem)
    fetch.start()
    packed = packed_ref[...]
    turned = packed.T
    row = lax.broadcasted_iota(jnp.int32, (S, S), 0)
    lane = lax.broadcasted_iota(jnp.int32, (S, S), 1)
    upper = lane > row
    diag = lane == row
    sym = jnp.where(upper, turned, packed) / snap_total
    skew = jnp.where(upper, packed, -turned) / snap_total
    hr_ref[...] = sym + jnp.where(diag, loading_level, 0.0)
    hi_ref[...] = jnp.where(diag, 0.0, skew)
    invert_hermitian(hr_ref, hi_ref)
    vr, vi = steer_ref[0:S], steer_ref[S : 2 * S]
    both = jnp.concatenate([vr, vi], axis=1)
    by_real = jnp.dot(hr_ref[...], both, precision=HIGHEST, preferred_element_type=jnp.float32)
    by_imag = jnp.dot(hi_ref[...], both, precision=HIGHEST, preferred_element_type=jnp.float32)
    wr = by_real[:, :B] - by_imag[:, B:]
    wi = by_real[:, B:] + by_imag[:, :B]
    power = jnp.sum(vr * wr + vi * wi, axis=0, keepdims=True)
    scale = 1.0 / jnp.sqrt(power)
    wr = (wr * scale).astype(jnp.bfloat16)
    wi = (wi * scale).astype(jnp.bfloat16)
    weights = jnp.concatenate([wr, wi], axis=0)
    swapped = jnp.concatenate([-wi, wr], axis=0)
    mix = jnp.concatenate([weights, swapped], axis=1).T
    width = 512
    fetch.wait()

    def tile(n, carry):
        at = pl.ds(pl.multiple_of(n * width, width), width)
        res = jnp.dot(mix, stacked_ref[:, at], preferred_element_type=jnp.float32)
        out_ref[:, at] = res.astype(jnp.bfloat16)
        return carry

    lax.fori_loop(0, stacked_ref.shape[1] // width, tile, 0)


def beams(packed, steer, stacked, snap_total):
    vmem = pl.BlockSpec(memory_space=pltpu.VMEM)
    return pl.pallas_call(
        functools.partial(beam_kernel, snap_total),
        out_shape=jax.ShapeDtypeStruct((2 * B, stacked.shape[1]), jnp.bfloat16),
        in_specs=[vmem, vmem, pl.BlockSpec(memory_space=pl.ANY)],
        out_specs=vmem,
        scratch_shapes=[
            pltpu.VMEM((S, S), jnp.float32),
            pltpu.VMEM((S, S), jnp.float32),
            pltpu.VMEM(stacked.shape, jnp.bfloat16),
            pltpu.SemaphoreType.DMA,
        ],
        name="beams",
    )(packed, steer, stacked)


def on_device(voltages, filter_taps, positions, beam_dirs, chan_table):
    snap_count = voltages.shape[2]
    packed, steer, stacked = front(voltages, filter_taps, positions, beam_dirs, chan_table)
    beam_out = beams(
        packed.reshape(S, S), steer, stacked.reshape(2 * S, snap_count), float(snap_count * SEG)
    )
    return beam_out.reshape(1, 2, B, snap_count)


def solution(mesh):
    return jax.shard_map(
        on_device,
        mesh=mesh,
        in_specs=(P("stn", None, "seg"), P(), P(), P(), P()),
        out_specs=P("stn", None, None, "seg"),
        check_vma=False,
    )
```

```python
import functools
import math

import jax
import jax.numpy as jnp
from jax import lax
from jax.experimental import pallas as pl
from jax.experimental.pallas import tpu as pltpu
from jax.sharding import PartitionSpec as P

C = 16
TAPS = 8
B = 128
DIRS = 360
S = 128
SEG = 16
STN = 16
CHUNKS = 4
PAD = 128
TILE = 512


loading_level = 0.1
full_turn = 2.0 * math.pi
HIGHEST = lax.Precision.HIGHEST
MESH = pl.DeviceIdType.MESH


def lane_of(value, i):
    return jnp.broadcast_to(value[:, i : i + 1], value.shape)


def row_of(value, i):
    return jnp.broadcast_to(value[i : i + 1, :], value.shape)


def parts(value):
    first = value.astype(jnp.bfloat16).astype(jnp.float32)
    rest = value - first
    second = rest.astype(jnp.bfloat16).astype(jnp.float32)
    return first, second, rest - second


def eliminate(pr, pi, base, row, lane):
    cr = [lane_of(pr, base + i) for i in range(8)]
    ci = [lane_of(pi, base + i) for i in range(8)]
    for i in range(8):
        inv = 1.0 / row_of(cr[i], i)
        here = row == i
        at = lane == base + i
        rr = jnp.where(at, inv, row_of(pr, i) * inv)
        ri = jnp.where(at, 0.0, row_of(pi, i) * inv)
        nr = jnp.where(at, 0.0, pr) - (cr[i] * rr - ci[i] * ri)
        ni = jnp.where(at, 0.0, pi) - (cr[i] * ri + ci[i] * rr)
        pr = jnp.where(here, rr, nr)
        pi = jnp.where(here, ri, ni)
        for j in range(i + 1, 8):
            mr = row_of(cr[j], i) * inv
            mi = row_of(ci[j], i) * inv
            nr = cr[j] - (cr[i] * mr - ci[i] * mi)
            ni = ci[j] - (cr[i] * mi + ci[i] * mr)
            cr[j] = jnp.where(here, mr, nr)
            ci[j] = jnp.where(here, mi, ni)
    return pr, pi


def invert_hermitian(hr_ref, hi_ref):
    count = S // 8
    lane = lax.broadcasted_iota(jnp.int32, (8, S), 1)
    row = lax.broadcasted_iota(jnp.int32, (8, S), 0)

    def inside(k):
        return (lane >= 8 * k) & (lane < 8 * k + 8)

    def load(g):
        return hr_ref[8 * g : 8 * g + 8, :], hi_ref[8 * g : 8 * g + 8, :]

    def store(g, ar, ai):
        hr_ref[8 * g : 8 * g + 8, :] = ar
        hi_ref[8 * g : 8 * g + 8, :] = ai

    def columns(k, panel):
        pieces = []
        for value in panel:
            value = jnp.where(lane < 8 * k, -value, jnp.where(inside(k), 0.0, value))
            a, b, c = parts(value)
            pieces += [a, a, b, b, a, c]
        return jnp.concatenate(pieces, axis=0).astype(jnp.bfloat16)

    def update(cols, panel):
        ra, rb, rc = parts(panel[0])
        ia, ib, ic = parts(panel[1])
        left = [ra, rb, ra, rb, rc, ra, ia, ib, ia, ib, ic, ia]
        right = [ia, ib, ia, ib, ic, ia, -ra, -rb, -ra, -rb, -rc, -ra]
        rows = jnp.concatenate(
            [jnp.concatenate(left, axis=0), jnp.concatenate(right, axis=0)], axis=1
        ).astype(jnp.bfloat16)
        return lax.dot_general(
            cols, rows, (((0,), (0,)), ((), ())), preferred_element_type=jnp.float32
        )

    def bulk(k, cols, panel, skip):
        term = update(cols, panel)
        for g in range(count):
            if g == k:
                store(g, *panel)
            elif g != skip:
                ar, ai = load(g)
                ar = jnp.where(inside(k), 0.0, ar) - term[8 * g : 8 * g + 8, :S]
                ai = jnp.where(inside(k), 0.0, ai) - term[8 * g : 8 * g + 8, S:]
                store(g, ar, ai)

    panel = load(0)
    cols = last = None
    for k in range(count):
        if k > 0:
            bulk(k - 1, cols, last, k)
        cols = columns(k, panel)
        last = eliminate(*panel, 8 * k, row, lane)
        if k + 1 < count:
            hr, hi = load(k + 1)
            ar = jnp.where(inside(k), 0.0, hr)
            ai = jnp.where(inside(k), 0.0, hi)
            for i in range(8):
                cr, ci = lane_of(hr, 8 * k + i), lane_of(hi, 8 * k + i)
                rr, ri = row_of(last[0], i), row_of(last[1], i)
                ar = ar - (cr * rr - ci * ri)
                ai = ai - (cr * ri + ci * rr)
            panel = ar, ai
    bulk(count - 1, cols, last, None)


def beam_kernel(snap_total, packed_ref, steer_ref, held_ref, out_ref, hr_ref, hi_ref, beam_ref, sem):
    packed = packed_ref[...].reshape(S, S)
    turned = packed.T
    row = lax.broadcasted_iota(jnp.int32, (S, S), 0)
    lane = lax.broadcasted_iota(jnp.int32, (S, S), 1)
    upper, diag = lane > row, lane == row
    sym = jnp.where(upper, turned, packed) / snap_total
    skew = jnp.where(upper, packed, -turned) / snap_total
    hr_ref[...] = sym + jnp.where(diag, loading_level, 0.0)
    hi_ref[...] = jnp.where(diag, 0.0, skew)
    invert_hermitian(hr_ref, hi_ref)
    vr, vi = steer_ref[0:S], steer_ref[S : 2 * S]
    both = jnp.concatenate([vr, vi], axis=1)
    by_real = jnp.dot(hr_ref[...], both, precision=HIGHEST, preferred_element_type=jnp.float32)
    by_imag = jnp.dot(hi_ref[...], both, precision=HIGHEST, preferred_element_type=jnp.float32)
    wr = by_real[:, :B] - by_imag[:, B:]
    wi = by_real[:, B:] + by_imag[:, :B]
    power = jnp.sum(vr * wr + vi * wi, axis=0, keepdims=True)
    scale = 1.0 / jnp.sqrt(power)
    wr = (wr * scale).astype(jnp.bfloat16)
    wi = (wi * scale).astype(jnp.bfloat16)
    weights = jnp.concatenate([wr, wi], axis=0)
    swapped = jnp.concatenate([-wi, wr], axis=0)
    mix = jnp.concatenate([weights, swapped], axis=1).T
    snaps = out_ref.shape[1]
    copies = []
    for n in range(snaps // TILE):
        at = pl.ds(n * TILE, TILE)
        block = held_ref[:, :, :, at].reshape(2 * S, TILE)
        res = jnp.dot(mix, block, preferred_element_type=jnp.float32)
        beam_ref[:, at] = res.astype(jnp.bfloat16)
        copy = pltpu.make_async_copy(beam_ref.at[:, at], out_ref.at[:, at], sem.at[n])
        copy.start()
        copies.append(copy)
    for copy in copies:
        copy.wait()


def beams(packed, steer, held, snap_total):
    vmem = pl.BlockSpec(memory_space=pltpu.VMEM)
    snaps = held.shape[3]
    return pl.pallas_call(
        functools.partial(beam_kernel, snap_total),
        out_shape=jax.ShapeDtypeStruct((2 * B, snaps), jnp.bfloat16),
        in_specs=[vmem, vmem, vmem],
        out_specs=pl.BlockSpec(memory_space=pltpu.HBM),
        scratch_shapes=[
            pltpu.VMEM((S, S), jnp.float32),
            pltpu.VMEM((S, S), jnp.float32),
            pltpu.VMEM((2 * B, snaps), jnp.bfloat16),
            pltpu.SemaphoreType.DMA((snaps // TILE,)),
        ],
        compiler_params=pltpu.CompilerParams(vmem_limit_bytes=16 * 1024 * 1024),
        name="beams",
    )(packed, steer, held)


def front_kernel(
    v_ref, taps_in, pos_in, dirs_in, chan_in,
    packed_ref, steer_ref, land,
    taps_ref, pos_ref, dirs_ref, chan_ref,
    vbuf, spread, spec, gram, part, landed,
    asem, vsem, hsem, send_x, recv_x, send_a, recv_a, send_b, recv_b,
):
    stn, seg = lax.axis_index("stn"), lax.axis_index("seg")
    stn_peers = [lax.rem(stn + d, STN) for d in range(1, STN)]
    seg_peers = [lax.rem(seg + d, SEG) for d in range(1, SEG)]
    local = v_ref.shape[0]
    snaps = v_ref.shape[2]
    wide = snaps // CHUNKS
    frame = 2 * C

    barrier = pltpu.get_barrier_semaphore()
    for peer in stn_peers:
        pl.semaphore_signal(barrier, inc=1, device_id={"stn": peer}, device_id_type=MESH)
    for peer in seg_peers:
        pl.semaphore_signal(barrier, inc=1, device_id={"seg": peer}, device_id_type=MESH)
    small = []
    for n, (src, dst) in enumerate(
        ((chan_in, chan_ref), (taps_in, taps_ref), (pos_in, pos_ref), (dirs_in, dirs_ref))
    ):
        fetch = pltpu.make_async_copy(src, dst, asem.at[n])
        fetch.start()
        small.append(fetch)
    fetches = []
    for c in range(CHUNKS):
        fetch = pltpu.make_async_copy(
            v_ref.at[:, :, pl.ds(c * wide, wide)],
            vbuf.at[:, :, pl.ds(PAD + c * wide, wide)],
            vsem.at[c],
        )
        fetch.start()
        fetches.append(fetch)

    for fetch in small:
        fetch.wait()
    row = lax.broadcasted_iota(jnp.int32, (frame, TAPS * frame), 0)
    lane = lax.broadcasted_iota(jnp.int32, (frame, TAPS * frame), 1)
    channel_of = jnp.zeros((frame, TAPS * frame), jnp.int32)
    for j in range(C):
        channel_of = jnp.where(row // 2 == j, chan_ref[j], channel_of)
    phase_index = jnp.bitwise_and(channel_of * jnp.bitwise_and(lane, frame - 1), frame - 1)
    angles = phase_index.astype(jnp.float32) * (full_turn / frame)
    table = jnp.where(row % 2 == 0, jnp.cos(angles), -jnp.sin(angles))
    taps = jnp.concatenate([taps_ref[m : m + 1, :] for m in range(TAPS)], axis=1)
    mixed = table * taps
    high = mixed.astype(jnp.bfloat16)
    low = (mixed - high.astype(jnp.float32)).astype(jnp.bfloat16)
    mixed = jnp.concatenate([high, low], axis=0)

    def channelize_chunk(c):
        def station(s, carry):
            x = vbuf[s, :, pl.ds(c * wide, wide + PAD)]
            moved = [x[:, PAD - m : PAD - m + wide] for m in range(TAPS)]
            res = jnp.dot(
                mixed, jnp.concatenate(moved, axis=0), preferred_element_type=jnp.float32
            )
            res = res[:frame] + res[frame:]
            for q in range(wide // PAD):
                spread[q, pl.ds(pl.multiple_of(s * frame, frame), frame), :] = res[
                    :, q * PAD : (q + 1) * PAD
                ]
            return carry

        lax.fori_loop(0, local, station, 0, unroll=2)
        for j in range(C):
            for a in range(2):
                for q in range(wide // PAD):
                    picked = spread[q, pl.ds(2 * j + a, local, stride=frame), :]
                    spec[c, j, a, :, q * PAD : (q + 1) * PAD] = picked.astype(jnp.bfloat16)

    def send_chunk(c):
        copies = []
        for d, peer in enumerate(stn_peers):
            copy = pltpu.make_async_remote_copy(
                src_ref=spec.at[c, peer],
                dst_ref=land.at[:, stn, :, pl.ds(c * wide, wide)],
                send_sem=send_x.at[c, d],
                recv_sem=recv_x.at[c, d],
                device_id={"stn": peer},
                device_id_type=MESH,
            )
            copy.start()
            copies.append(copy)
        land[:, stn, :, pl.ds(c * wide, wide)] = spec[c, stn]
        return copies

    order = list(range(1, CHUNKS)) + [0]
    for c in range(2):
        fetches[c].wait()
    channelize_chunk(order[0])
    pl.semaphore_wait(barrier, STN - 1 + SEG - 1)
    halo = pltpu.make_async_remote_copy(
        src_ref=v_ref.at[:, :, pl.ds(snaps - PAD, PAD)],
        dst_ref=vbuf.at[:, :, pl.ds(0, PAD)],
        send_sem=hsem.at[0],
        recv_sem=hsem.at[1],
        device_id={"seg": seg_peers[0]},
        device_id_type=MESH,
    )
    halo.start()
    sent = {order[0]: send_chunk(order[0])}
    for c in order[1:]:
        if c >= 2:
            fetches[c].wait()
        if c == 0:
            halo.wait()

            @pl.when(seg == 0)
            def _():
                vbuf[:, :, 0:PAD] = jnp.zeros((local, frame, PAD), jnp.bfloat16)

        channelize_chunk(c)
        sent[c] = send_chunk(c)

    bearing = dirs_ref[...].astype(jnp.float32) * (full_turn / DIRS)
    frequency = 1.0 + chan_ref[stn].astype(jnp.float32) / C
    east = jnp.broadcast_to(pos_ref[0:1, :], (S, S)).T
    north = jnp.broadcast_to(pos_ref[1:2, :], (S, S)).T
    phases = (full_turn * frequency) * (east * jnp.cos(bearing) + north * jnp.sin(bearing))
    steer_ref[0:S, :] = jnp.cos(phases)
    steer_ref[S : 2 * S, :] = jnp.sin(phases)

    for n, c in enumerate(order):
        for copy in sent[c]:
            copy.wait_recv()
        at = pl.ds(c * wide, wide)
        block = land[:, :, :, at].reshape(2 * S, wide)
        term = lax.dot_general(
            block, block, (((1,), (1,)), ((), ())), preferred_element_type=jnp.float32
        )
        if n == 0:
            gram[...] = term
        else:
            gram[...] += term

    sym = gram[0:S, 0:S] + gram[S : 2 * S, S : 2 * S]
    skew = gram[S : 2 * S, 0:S] - gram[0:S, S : 2 * S]
    row = lax.broadcasted_iota(jnp.int32, (S, S), 0)
    lane = lax.broadcasted_iota(jnp.int32, (S, S), 1)
    part[...] = jnp.where(lane > row, skew, sym).reshape(part.shape)

    spread_out = []
    for d, peer in enumerate(seg_peers):
        copy = pltpu.make_async_remote_copy(
            src_ref=part.at[peer],
            dst_ref=landed.at[d],
            send_sem=send_a.at[d],
            recv_sem=recv_a.at[d],
            device_id={"seg": peer},
            device_id_type=MESH,
        )
        copy.start()
        spread_out.append(copy)
    total = part[seg]
    for d, copy in enumerate(spread_out):
        copy.wait_recv()
        total = total + landed[d]
    packed_ref[seg] = total
    shared = []
    for d, peer in enumerate(seg_peers):
        copy = pltpu.make_async_remote_copy(
            src_ref=packed_ref.at[seg],
            dst_ref=packed_ref.at[seg],
            send_sem=send_b.at[d],
            recv_sem=recv_b.at[d],
            device_id={"seg": peer},
            device_id_type=MESH,
        )
        copy.start()
        shared.append(copy)
    for c in order:
        for copy in sent[c]:
            copy.wait_send()
    for copy in spread_out:
        copy.wait_send()
    for copy in shared:
        copy.wait()


def front(voltages, filter_taps, positions, beam_dirs, chan_table):
    local, frame, snaps = voltages.shape
    wide = snaps // CHUNKS
    rows = S // SEG
    vmem = pl.BlockSpec(memory_space=pltpu.VMEM)
    hbm = pl.BlockSpec(memory_space=pltpu.HBM)
    dma = pltpu.SemaphoreType.DMA
    return pl.pallas_call(
        front_kernel,
        out_shape=(
            jax.ShapeDtypeStruct((SEG, rows, S), jnp.float32),
            jax.ShapeDtypeStruct((2 * S, B), jnp.float32),
            jax.ShapeDtypeStruct((2, STN, local, snaps), jnp.bfloat16),
        ),
        in_specs=[hbm] * 5,
        out_specs=(vmem, vmem, vmem),
        scratch_shapes=[
            pltpu.VMEM(filter_taps.shape, jnp.float32),
            pltpu.VMEM(positions.shape, jnp.float32),
            pltpu.VMEM((1, B), jnp.int32),
            pltpu.SMEM(chan_table.shape, jnp.int32),
            pltpu.VMEM((local, frame, PAD + snaps), jnp.bfloat16),
            pltpu.VMEM((wide // PAD, local * frame, PAD), jnp.float32),
            pltpu.VMEM((CHUNKS, STN, 2, local, wide), jnp.bfloat16),
            pltpu.VMEM((2 * S, 2 * S), jnp.float32),
            pltpu.VMEM((SEG, rows, S), jnp.float32),
            pltpu.VMEM((SEG - 1, rows, S), jnp.float32),
            dma((4,)),
            dma((CHUNKS,)),
            dma((2,)),
            dma((CHUNKS, STN - 1)),
            dma((CHUNKS, STN - 1)),
            dma((SEG - 1,)),
            dma((SEG - 1,)),
            dma((SEG - 1,)),
            dma((SEG - 1,)),
        ],
        compiler_params=pltpu.CompilerParams(
            collective_id=1, has_side_effects=True, vmem_limit_bytes=48_000_000
        ),
        name="front",
    )(voltages, filter_taps, positions, beam_dirs, chan_table)


def on_device(voltages, filter_taps, positions, beam_dirs, chan_table):
    snap_count = voltages.shape[2]
    stay = lambda x: pltpu.with_memory_space_constraint(x, pltpu.HBM)
    packed, steer, held = front(stay(voltages), stay(filter_taps), stay(positions), stay(beam_dirs.reshape(1, B)), stay(chan_table))
    beam_out = beams(packed, steer, held, float(snap_count * SEG))
    return beam_out.reshape(1, 2, B, snap_count)


def solution(mesh):
    return jax.shard_map(
        on_device,
        mesh=mesh,
        in_specs=(P("stn", None, "seg"), P(), P(), P(), P()),
        out_specs=P("stn", None, None, "seg"),
        check_vma=False,
    )
```

```python
import functools
import math

import jax
import jax.numpy as jnp
from jax import lax
from jax.experimental import pallas as pl
from jax.experimental.pallas import tpu as pltpu
from jax.sharding import PartitionSpec as P

C = 16
TAPS = 8
B = 128
DIRS = 360
S = 128
SEG = 16
STN = 16
PIECE = 512
ORDER = ((1536, 512), (512, 1024), (0, 512))
PAD = 128
TILE = 512
SIDE = 4


loading_level = 0.1
full_turn = 2.0 * math.pi
HIGHEST = lax.Precision.HIGHEST
MESH = pl.DeviceIdType.MESH


def lane_of(value, i):
    return jnp.broadcast_to(value[:, i : i + 1], value.shape)


def row_of(value, i):
    return jnp.broadcast_to(value[i : i + 1, :], value.shape)


def parts(value):
    first = value.astype(jnp.bfloat16).astype(jnp.float32)
    rest = value - first
    second = rest.astype(jnp.bfloat16).astype(jnp.float32)
    return first, second, rest - second


def eliminate(pr, pi, base, row, lane):
    cr = [lane_of(pr, base + i) for i in range(8)]
    ci = [lane_of(pi, base + i) for i in range(8)]
    for i in range(8):
        inv = 1.0 / row_of(cr[i], i)
        here = row == i
        at = lane == base + i
        rr = jnp.where(at, inv, row_of(pr, i) * inv)
        ri = jnp.where(at, 0.0, row_of(pi, i) * inv)
        nr = jnp.where(at, 0.0, pr) - (cr[i] * rr - ci[i] * ri)
        ni = jnp.where(at, 0.0, pi) - (cr[i] * ri + ci[i] * rr)
        pr = jnp.where(here, rr, nr)
        pi = jnp.where(here, ri, ni)
        for j in range(i + 1, 8):
            mr = row_of(cr[j], i) * inv
            mi = row_of(ci[j], i) * inv
            nr = cr[j] - (cr[i] * mr - ci[i] * mi)
            ni = ci[j] - (cr[i] * mi + ci[i] * mr)
            cr[j] = jnp.where(here, mr, nr)
            ci[j] = jnp.where(here, mi, ni)
    return pr, pi


def invert_hermitian(hr_ref, hi_ref):
    count = S // 8
    lane = lax.broadcasted_iota(jnp.int32, (8, S), 1)
    row = lax.broadcasted_iota(jnp.int32, (8, S), 0)

    def inside(k):
        return (lane >= 8 * k) & (lane < 8 * k + 8)

    def load(g):
        return hr_ref[8 * g : 8 * g + 8, :], hi_ref[8 * g : 8 * g + 8, :]

    def store(g, ar, ai):
        hr_ref[8 * g : 8 * g + 8, :] = ar
        hi_ref[8 * g : 8 * g + 8, :] = ai

    def columns(k, panel):
        pieces = []
        for value in panel:
            value = jnp.where(lane < 8 * k, -value, jnp.where(inside(k), 0.0, value))
            a, b, c = parts(value)
            pieces += [a, a, b, b, a, c]
        return jnp.concatenate(pieces, axis=0).astype(jnp.bfloat16)

    def update(cols, panel):
        ra, rb, rc = parts(panel[0])
        ia, ib, ic = parts(panel[1])
        left = [ra, rb, ra, rb, rc, ra, ia, ib, ia, ib, ic, ia]
        right = [ia, ib, ia, ib, ic, ia, -ra, -rb, -ra, -rb, -rc, -ra]
        rows = jnp.concatenate(
            [jnp.concatenate(left, axis=0), jnp.concatenate(right, axis=0)], axis=1
        ).astype(jnp.bfloat16)
        return lax.dot_general(
            cols, rows, (((0,), (0,)), ((), ())), preferred_element_type=jnp.float32
        )

    def bulk(k, cols, panel, skip):
        term = update(cols, panel)
        for g in range(count):
            if g == k:
                store(g, *panel)
            elif g != skip:
                ar, ai = load(g)
                ar = jnp.where(inside(k), 0.0, ar) - term[8 * g : 8 * g + 8, :S]
                ai = jnp.where(inside(k), 0.0, ai) - term[8 * g : 8 * g + 8, S:]
                store(g, ar, ai)

    panel = load(0)
    cols = last = None
    for k in range(count):
        if k > 0:
            bulk(k - 1, cols, last, k)
        cols = columns(k, panel)
        last = eliminate(*panel, 8 * k, row, lane)
        if k + 1 < count:
            hr, hi = load(k + 1)
            ar = jnp.where(inside(k), 0.0, hr)
            ai = jnp.where(inside(k), 0.0, hi)
            for i in range(8):
                cr, ci = lane_of(hr, 8 * k + i), lane_of(hi, 8 * k + i)
                rr, ri = row_of(last[0], i), row_of(last[1], i)
                ar = ar - (cr * rr - ci * ri)
                ai = ai - (cr * ri + ci * rr)
            panel = ar, ai
    bulk(count - 1, cols, last, None)


def beam_kernel(snap_total, packed_ref, steer_ref, *refs):
    held, (out_ref, hr_ref, hi_ref, beam_ref, sem) = refs[: len(ORDER)], refs[len(ORDER) :]
    packed = packed_ref[...].reshape(S, S)
    turned = packed.T
    row = lax.broadcasted_iota(jnp.int32, (S, S), 0)
    lane = lax.broadcasted_iota(jnp.int32, (S, S), 1)
    upper, diag = lane > row, lane == row
    sym = jnp.where(upper, turned, packed) / snap_total
    skew = jnp.where(upper, packed, -turned) / snap_total
    hr_ref[...] = sym + jnp.where(diag, loading_level, 0.0)
    hi_ref[...] = jnp.where(diag, 0.0, skew)
    invert_hermitian(hr_ref, hi_ref)
    vr, vi = steer_ref[0:S], steer_ref[S : 2 * S]
    both = jnp.concatenate([vr, vi], axis=1)
    by_real = jnp.dot(hr_ref[...], both, precision=HIGHEST, preferred_element_type=jnp.float32)
    by_imag = jnp.dot(hi_ref[...], both, precision=HIGHEST, preferred_element_type=jnp.float32)
    wr = by_real[:, :B] - by_imag[:, B:]
    wi = by_real[:, B:] + by_imag[:, :B]
    power = jnp.sum(vr * wr + vi * wi, axis=0, keepdims=True)
    scale = 1.0 / jnp.sqrt(power)
    wr = (wr * scale).astype(jnp.bfloat16)
    wi = (wi * scale).astype(jnp.bfloat16)
    weights = jnp.concatenate([wr, wi], axis=0)
    swapped = jnp.concatenate([-wi, wr], axis=0)
    mix = jnp.concatenate([weights, swapped], axis=1).T
    copies = []
    for ref, (start, wide) in zip(held, ORDER):
        for n in range(0, wide, TILE):
            width = min(TILE, wide)
            res = jnp.dot(
                mix, stacked(ref, slice(n, n + width)), preferred_element_type=jnp.float32
            )
            at = pl.ds(start + n, width)
            beam_ref[:, at] = res.astype(jnp.bfloat16)
            copy = pltpu.make_async_copy(
                beam_ref.at[:, at], out_ref.at[:, at], sem.at[len(copies)]
            )
            copy.start()
            copies.append(copy)
    for copy in copies:
        copy.wait()


def beams(packed, steer, held, snaps):
    vmem = pl.BlockSpec(memory_space=pltpu.VMEM)
    return pl.pallas_call(
        functools.partial(beam_kernel, float(snaps * SEG)),
        out_shape=jax.ShapeDtypeStruct((2 * B, snaps), jnp.bfloat16),
        in_specs=[vmem] * (2 + len(ORDER)),
        out_specs=pl.BlockSpec(memory_space=pltpu.HBM),
        scratch_shapes=[
            pltpu.VMEM((S, S), jnp.float32),
            pltpu.VMEM((S, S), jnp.float32),
            pltpu.VMEM((2 * B, snaps), jnp.bfloat16),
            pltpu.SemaphoreType.DMA((snaps // TILE,)),
        ],
        compiler_params=pltpu.CompilerParams(vmem_limit_bytes=16 * 1024 * 1024),
        name="beams",
    )(packed, steer, *held)


def stacked(ref, at=slice(None)):
    both = jnp.concatenate([ref[:, 0, :, at], ref[:, 1, :, at]], axis=0)
    return both.reshape(2 * S, both.shape[2])


def front_kernel(v_ref, taps_in, pos_in, dirs_in, chan_in, packed_ref, steer_ref, *refs):
    held, refs = refs[: len(ORDER)], refs[len(ORDER) :]
    specs, refs = refs[: len(ORDER)], refs[len(ORDER) :]
    (
        taps_ref, pos_ref, dirs_ref, chan_ref,
        vbuf, spread, gram, part, landed, middle, landed_b,
        asem, vsem, hsem, send_x, recv_x, send_a, recv_a,
    ) = refs
    stn, seg = lax.axis_index("stn"), lax.axis_index("seg")
    stn_peers = [lax.rem(stn + d, STN) for d in (8, 7, 9, 6, 10, 5, 11, 4, 12, 3, 13, 2, 14, 1, 15)]
    seg_peers = [lax.rem(seg + d, SEG) for d in range(1, SEG)]
    local = v_ref.shape[0]
    snaps = v_ref.shape[2]
    frame = 2 * C

    barrier = pltpu.get_barrier_semaphore()
    for peer in stn_peers:
        pl.semaphore_signal(barrier, inc=1, device_id={"stn": peer}, device_id_type=MESH)
    for peer in seg_peers:
        pl.semaphore_signal(barrier, inc=1, device_id={"seg": peer}, device_id_type=MESH)
    small = []
    for n, (src, dst) in enumerate(
        ((chan_in, chan_ref), (taps_in, taps_ref), (pos_in, pos_ref), (dirs_in, dirs_ref))
    ):
        fetch = pltpu.make_async_copy(src, dst, asem.at[n])
        fetch.start()
        small.append(fetch)
    pending = {}
    for start, wide in ORDER:
        for n in range((start + wide) // PIECE - 1, max(start - PAD, 0) // PIECE - 1, -1):
            if n not in pending:
                fetch = pltpu.make_async_copy(
                    v_ref.at[:, :, pl.ds(n * PIECE, PIECE)],
                    vbuf.at[:, :, pl.ds(PAD + n * PIECE, PIECE)],
                    vsem.at[n],
                )
                fetch.start()
                pending[n] = fetch

    for fetch in small:
        fetch.wait()
    row = lax.broadcasted_iota(jnp.int32, (frame, TAPS * frame), 0)
    lane = lax.broadcasted_iota(jnp.int32, (frame, TAPS * frame), 1)
    channel_of = jnp.zeros((frame, TAPS * frame), jnp.int32)
    for j in range(C):
        channel_of = jnp.where(row // 2 == j, chan_ref[j], channel_of)
    phase_index = jnp.bitwise_and(channel_of * jnp.bitwise_and(lane, frame - 1), frame - 1)
    angles = phase_index.astype(jnp.float32) * (full_turn / frame)
    table = jnp.where(row % 2 == 0, jnp.cos(angles), -jnp.sin(angles))
    taps = jnp.concatenate([taps_ref[m : m + 1, :] for m in range(TAPS)], axis=1)
    mixed = table * taps
    high = mixed.astype(jnp.bfloat16)
    low = (mixed - high.astype(jnp.float32)).astype(jnp.bfloat16)
    mixed = jnp.concatenate([high, low], axis=0)

    def channelize_chunk(c):
        start, wide = ORDER[c]
        for n in sorted(pending):
            if n * PIECE < start + wide and (n + 1) * PIECE > start - PAD:
                pending.pop(n).wait()

        def station(s, carry):
            x = vbuf[s, :, pl.ds(start, wide + PAD)]
            for q in range(0, wide, PIECE):
                width = min(PIECE, wide)
                moved = [x[:, PAD - m + q : PAD - m + q + width] for m in range(TAPS)]
                res = jnp.dot(
                    mixed, jnp.concatenate(moved, axis=0), preferred_element_type=jnp.float32
                )
                res = res[:frame] + res[frame:]
                for t in range(width // PAD):
                    spread[q // PAD + t, pl.ds(pl.multiple_of(s * frame, frame), frame), :] = res[
                        :, t * PAD : (t + 1) * PAD
                    ]
            return carry

        lax.fori_loop(0, local, station, 0, unroll=2)
        for q in range(wide // PAD):
            for j in range(C):
                for a in range(2):
                    picked = spread[q, pl.ds(2 * j + a, local, stride=frame), :]
                    specs[c][j, a, :, q * PAD : (q + 1) * PAD] = picked.astype(jnp.bfloat16)

    def send_chunk(c):
        copies = []
        for d, peer in enumerate(stn_peers):
            copy = pltpu.make_async_remote_copy(
                src_ref=specs[c].at[peer],
                dst_ref=held[c].at[stn],
                send_sem=send_x.at[c, d],
                recv_sem=recv_x.at[c, d],
                device_id={"stn": peer},
                device_id_type=MESH,
            )
            copy.start()
            copies.append(copy)
        held[c][stn] = specs[c][stn]
        return copies

    channelize_chunk(0)
    pl.semaphore_wait(barrier, STN - 1 + SEG - 1)
    halo = pltpu.make_async_remote_copy(
        src_ref=v_ref.at[:, :, pl.ds(snaps - PAD, PAD)],
        dst_ref=vbuf.at[:, :, pl.ds(0, PAD)],
        send_sem=hsem.at[0],
        recv_sem=hsem.at[1],
        device_id={"seg": lax.rem(seg + 1, SEG)},
        device_id_type=MESH,
    )
    halo.start()
    sent = [send_chunk(0)]
    for c in range(1, len(ORDER)):
        if ORDER[c][0] == 0:
            halo.wait()

            @pl.when(seg == 0)
            def _():
                vbuf[:, :, 0:PAD] = jnp.zeros((local, frame, PAD), jnp.bfloat16)

        channelize_chunk(c)
        sent.append(send_chunk(c))

    bearing = dirs_ref[...].astype(jnp.float32) * (full_turn / DIRS)
    frequency = 1.0 + chan_ref[stn].astype(jnp.float32) / C
    east = jnp.broadcast_to(pos_ref[0:1, :], (S, S)).T
    north = jnp.broadcast_to(pos_ref[1:2, :], (S, S)).T
    phases = (full_turn * frequency) * (east * jnp.cos(bearing) + north * jnp.sin(bearing))
    steer_ref[0:S, :] = jnp.cos(phases)
    steer_ref[S : 2 * S, :] = jnp.sin(phases)

    for n, copies in enumerate(sent):
        for copy in copies:
            copy.wait_recv()
        block = stacked(held[n])
        term = lax.dot_general(
            block, block, (((1,), (1,)), ((), ())), preferred_element_type=jnp.float32
        )
        if n == 0:
            gram[...] = term
        else:
            gram[...] += term

    sym = gram[0:S, 0:S] + gram[S : 2 * S, S : 2 * S]
    skew = gram[S : 2 * S, 0:S] - gram[0:S, S : 2 * S]
    row = lax.broadcasted_iota(jnp.int32, (S, S), 0)
    lane = lax.broadcasted_iota(jnp.int32, (S, S), 1)
    part[...] = jnp.where(lane > row, skew, sym).reshape(part.shape)

    across = [lax.rem(seg // SIDE + d, SIDE) * SIDE + lax.rem(seg, SIDE) for d in (2, 1, 3)]
    along = [seg // SIDE * SIDE + lax.rem(seg + d, SIDE) for d in (2, 1, 3)]
    half = SEG // 2

    def exchange(source, target, ways, n):
        copies = []
        for d in range(SIDE - 1):
            for h in range(2):
                copy = pltpu.make_async_remote_copy(
                    src_ref=source.at[pl.ds(h * half, half)],
                    dst_ref=target.at[d, pl.ds(h * half, half)],
                    send_sem=send_a.at[n, d, h],
                    recv_sem=recv_a.at[n, d, h],
                    device_id={"seg": ways[h][d]},
                    device_id_type=MESH,
                )
                copy.start()
                copies.append(copy)
        return copies

    first = exchange(part, landed, (along, across), 0)
    for h in range(2):
        for copy in first[h::2]:
            copy.wait_recv()
        at = pl.ds(h * half, half)
        middle[at] = part[at] + landed[0, at] + landed[1, at] + landed[2, at]
    second = exchange(middle, landed_b, (across, along), 1)
    for h in range(2):
        for copy in second[h::2]:
            copy.wait_recv()
        at = pl.ds(h * half, half)
        packed_ref[at] = middle[at] + landed_b[0, at] + landed_b[1, at] + landed_b[2, at]
    for copies in sent:
        for copy in copies:
            copy.wait_send()
    for copy in first + second:
        copy.wait_send()


def front(voltages, filter_taps, positions, beam_dirs, chan_table):
    local, frame, snaps = voltages.shape
    widths = [wide for _, wide in ORDER]
    rows = S // SEG
    vmem = pl.BlockSpec(memory_space=pltpu.VMEM)
    hbm = pl.BlockSpec(memory_space=pltpu.HBM)
    dma = pltpu.SemaphoreType.DMA
    return pl.pallas_call(
        front_kernel,
        out_shape=(
            jax.ShapeDtypeStruct((SEG, rows, S), jnp.float32),
            jax.ShapeDtypeStruct((2 * S, B), jnp.float32),
            *[jax.ShapeDtypeStruct((STN, 2, local, wide), jnp.bfloat16) for wide in widths],
        ),
        in_specs=[hbm] * 5,
        out_specs=(vmem,) * (2 + len(ORDER)),
        scratch_shapes=[
            *[pltpu.VMEM((STN, 2, local, wide), jnp.bfloat16) for wide in widths],
            pltpu.VMEM(filter_taps.shape, jnp.float32),
            pltpu.VMEM(positions.shape, jnp.float32),
            pltpu.VMEM((1, B), jnp.int32),
            pltpu.SMEM(chan_table.shape, jnp.int32),
            pltpu.VMEM((local, frame, PAD + snaps), jnp.bfloat16),
            pltpu.VMEM((max(widths) // PAD, local * frame, PAD), jnp.float32),
            pltpu.VMEM((2 * S, 2 * S), jnp.float32),
            pltpu.VMEM((SEG, rows, S), jnp.float32),
            pltpu.VMEM((SIDE - 1, SEG, rows, S), jnp.float32),
            pltpu.VMEM((SEG, rows, S), jnp.float32),
            pltpu.VMEM((SIDE - 1, SEG, rows, S), jnp.float32),
            dma((4,)),
            dma((snaps // PIECE,)),
            dma((2,)),
            dma((len(ORDER), STN - 1)),
            dma((len(ORDER), STN - 1)),
            dma((2, SIDE - 1, 2)),
            dma((2, SIDE - 1, 2)),
        ],
        compiler_params=pltpu.CompilerParams(
            collective_id=1, has_side_effects=True, vmem_limit_bytes=48_000_000
        ),
        name="front",
    )(voltages, filter_taps, positions, beam_dirs, chan_table)


def on_device(voltages, filter_taps, positions, beam_dirs, chan_table):
    snap_count = voltages.shape[2]
    stay = lambda x: pltpu.with_memory_space_constraint(x, pltpu.HBM)
    packed, steer, *held = front(stay(voltages), stay(filter_taps), stay(positions), stay(beam_dirs.reshape(1, B)), stay(chan_table))
    beam_out = beams(packed, steer, held, snap_count)
    return beam_out.reshape(1, 2, B, snap_count)


def solution(mesh):
    return jax.shard_map(
        on_device,
        mesh=mesh,
        in_specs=(P("stn", None, "seg"), P(), P(), P(), P()),
        out_specs=P("stn", None, None, "seg"),
        check_vma=False,
    )
```

```python
import functools
import math

import jax
import jax.numpy as jnp
from jax import lax
from jax.experimental import pallas as pl
from jax.experimental.pallas import tpu as pltpu
from jax.sharding import PartitionSpec as P

C = 16
TAPS = 8
B = 128
DIRS = 360
S = 128
SEG = 16
STN = 16
PIECE = 512
ORDER = ((1536, 512), (512, 1024), (0, 512))
PAD = 128
TILE = 512
SIDE = 4


loading_level = 0.1
full_turn = 2.0 * math.pi
HIGHEST = lax.Precision.HIGHEST
MESH = pl.DeviceIdType.MESH


def lane_of(value, i):
    return jnp.broadcast_to(value[:, i : i + 1], value.shape)


def row_of(value, i):
    return jnp.broadcast_to(value[i : i + 1, :], value.shape)


def parts(value):
    first = value.astype(jnp.bfloat16).astype(jnp.float32)
    rest = value - first
    second = rest.astype(jnp.bfloat16).astype(jnp.float32)
    return first, second, rest - second


def eliminate(pr, pi, base, row, lane):
    cr = [lane_of(pr, base + i) for i in range(8)]
    ci = [lane_of(pi, base + i) for i in range(8)]
    pivot = row_of(cr[0], 0)
    for i in range(8):
        inv = 1.0 / pivot
        if i < 7:
            br, bi = row_of(cr[i + 1], i), row_of(ci[i + 1], i)
            pivot = row_of(cr[i + 1], i + 1) - (br * br + bi * bi) * inv
        here = row == i
        gr = jnp.where(here, -1.0, cr[i]) * inv
        gi = jnp.where(here, 0.0, ci[i]) * inv
        for j in range(i + 1, 8):
            br, bi = row_of(cr[j], i), row_of(ci[j], i)
            cr[j] = jnp.where(here, 0.0, cr[j]) - (gr * br - gi * bi)
            ci[j] = jnp.where(here, 0.0, ci[j]) - (gr * bi + gi * br)
        at = lane == base + i
        br = jnp.where(at, 1.0, row_of(pr, i))
        bi = jnp.where(at, 0.0, row_of(pi, i))
        cross = here | at
        pr = jnp.where(cross, 0.0, pr) - (gr * br - gi * bi)
        pi = jnp.where(cross, 0.0, pi) - (gr * bi + gi * br)
    return pr, pi


def tree_sum(terms):
    while len(terms) > 1:
        terms = [a + b for a, b in zip(terms[::2], terms[1::2])]
    return terms[0]


def subtract_block(group, base, panel, lane):
    hr, hi = group
    inside = (lane >= base) & (lane < base + 8)
    real, imag = [], []
    for i in range(8):
        cr, ci = lane_of(hr, base + i), lane_of(hi, base + i)
        rr, ri = row_of(panel[0], i), row_of(panel[1], i)
        real.append(cr * rr - ci * ri)
        imag.append(cr * ri + ci * rr)
    return (
        jnp.where(inside, 0.0, hr) - tree_sum(real),
        jnp.where(inside, 0.0, hi) - tree_sum(imag),
    )


def invert_hermitian(hr_ref, hi_ref):
    count = S // 8
    lane = lax.broadcasted_iota(jnp.int32, (8, S), 1)
    row = lax.broadcasted_iota(jnp.int32, (8, S), 0)

    def inside(k):
        return (lane >= 8 * k) & (lane < 8 * k + 8)

    def load(g):
        return hr_ref[8 * g : 8 * g + 8, :], hi_ref[8 * g : 8 * g + 8, :]

    def store(g, ar, ai):
        hr_ref[8 * g : 8 * g + 8, :] = ar
        hi_ref[8 * g : 8 * g + 8, :] = ai

    def columns(k, panel):
        pieces = []
        for value in panel:
            value = jnp.where(lane < 8 * k, -value, jnp.where(inside(k), 0.0, value))
            a, b, c = parts(value)
            pieces += [a, a, b, b, a, c]
        return jnp.concatenate(pieces, axis=0).astype(jnp.bfloat16)

    def update(cols, panel):
        ra, rb, rc = parts(panel[0])
        ia, ib, ic = parts(panel[1])
        left = [ra, rb, ra, rb, rc, ra, ia, ib, ia, ib, ic, ia]
        right = [ia, ib, ia, ib, ic, ia, -ra, -rb, -ra, -rb, -rc, -ra]
        rows = jnp.concatenate(
            [jnp.concatenate(left, axis=0), jnp.concatenate(right, axis=0)], axis=1
        ).astype(jnp.bfloat16)
        return lax.dot_general(
            cols, rows, (((0,), (0,)), ((), ())), preferred_element_type=jnp.float32
        )

    def bulk(k, cols, panel, skip):
        term = update(cols, panel)
        for g in range(count):
            if g == k:
                store(g, *panel)
            elif g not in skip:
                ar, ai = load(g)
                ar = jnp.where(inside(k), 0.0, ar) - term[8 * g : 8 * g + 8, :S]
                ai = jnp.where(inside(k), 0.0, ai) - term[8 * g : 8 * g + 8, S:]
                store(g, ar, ai)

    panel = load(0)
    cols = last = None
    for k in range(count):
        if k > 0:
            bulk(k - 1, cols, last, (k,))
        ahead = load(k + 1) if k + 1 < count else None
        cols = columns(k, panel)
        last = eliminate(*panel, 8 * k, row, lane)
        if ahead is not None:
            panel = subtract_block(ahead, 8 * k, last, lane)
    bulk(count - 1, cols, last, ())


def beam_kernel(snap_total, packed_ref, steer_ref, *refs):
    held, (out_ref, hr_ref, hi_ref, beam_ref, sem) = refs[: len(ORDER)], refs[len(ORDER) :]
    packed = packed_ref[...].reshape(S, S)
    turned = packed.T
    row = lax.broadcasted_iota(jnp.int32, (S, S), 0)
    lane = lax.broadcasted_iota(jnp.int32, (S, S), 1)
    upper, diag = lane > row, lane == row
    sym = jnp.where(upper, turned, packed) / snap_total
    skew = jnp.where(upper, packed, -turned) / snap_total
    hr_ref[...] = sym + jnp.where(diag, loading_level, 0.0)
    hi_ref[...] = jnp.where(diag, 0.0, skew)
    invert_hermitian(hr_ref, hi_ref)
    vr, vi = steer_ref[0:S], steer_ref[S : 2 * S]
    both = jnp.concatenate([vr, vi], axis=1)
    by_real = jnp.dot(hr_ref[...], both, precision=HIGHEST, preferred_element_type=jnp.float32)
    by_imag = jnp.dot(hi_ref[...], both, precision=HIGHEST, preferred_element_type=jnp.float32)
    wr = by_real[:, :B] - by_imag[:, B:]
    wi = by_real[:, B:] + by_imag[:, :B]
    power = jnp.sum(vr * wr + vi * wi, axis=0, keepdims=True)
    scale = 1.0 / jnp.sqrt(power)
    wr = (wr * scale).astype(jnp.bfloat16)
    wi = (wi * scale).astype(jnp.bfloat16)
    weights = jnp.concatenate([wr, wi], axis=0)
    swapped = jnp.concatenate([-wi, wr], axis=0)
    mix = jnp.concatenate([weights, swapped], axis=1).T
    copies = []
    for ref, (start, wide) in zip(held, ORDER):
        for n in range(0, wide, TILE):
            width = min(TILE, wide)
            res = jnp.dot(
                mix, stacked(ref, slice(n, n + width)), preferred_element_type=jnp.float32
            )
            at = pl.ds(start + n, width)
            beam_ref[:, at] = res.astype(jnp.bfloat16)
            copy = pltpu.make_async_copy(
                beam_ref.at[:, at], out_ref.at[:, at], sem.at[len(copies)]
            )
            copy.start()
            copies.append(copy)
    for copy in copies:
        copy.wait()


def beams(packed, steer, held, snaps):
    vmem = pl.BlockSpec(memory_space=pltpu.VMEM)
    return pl.pallas_call(
        functools.partial(beam_kernel, float(snaps * SEG)),
        out_shape=jax.ShapeDtypeStruct((2 * B, snaps), jnp.bfloat16),
        in_specs=[vmem] * (2 + len(ORDER)),
        out_specs=pl.BlockSpec(memory_space=pltpu.HBM),
        scratch_shapes=[
            pltpu.VMEM((S, S), jnp.float32),
            pltpu.VMEM((S, S), jnp.float32),
            pltpu.VMEM((2 * B, snaps), jnp.bfloat16),
            pltpu.SemaphoreType.DMA((snaps // TILE,)),
        ],
        compiler_params=pltpu.CompilerParams(vmem_limit_bytes=16 * 1024 * 1024),
        name="beams",
    )(packed, steer, *held)


def stacked(ref, at=slice(None)):
    both = jnp.concatenate([ref[:, 0, :, at], ref[:, 1, :, at]], axis=0)
    return both.reshape(2 * S, both.shape[2])


def front_kernel(v_ref, taps_in, pos_in, dirs_in, chan_in, packed_ref, steer_ref, *refs):
    held, refs = refs[: len(ORDER)], refs[len(ORDER) :]
    specs, refs = refs[: len(ORDER)], refs[len(ORDER) :]
    (
        taps_ref, pos_ref, dirs_ref, chan_ref,
        vbuf, spread, gram, part, landed, middle, landed_b,
        asem, vsem, hsem, send_x, recv_x, send_a, recv_a,
    ) = refs
    stn, seg = lax.axis_index("stn"), lax.axis_index("seg")
    stn_peers = [lax.rem(stn + d, STN) for d in (8, 7, 9, 6, 10, 5, 11, 4, 12, 3, 13, 2, 14, 1, 15)]
    seg_peers = [lax.rem(seg + d, SEG) for d in range(1, SEG)]
    local = v_ref.shape[0]
    snaps = v_ref.shape[2]
    frame = 2 * C

    barrier = pltpu.get_barrier_semaphore()
    for peer in stn_peers:
        pl.semaphore_signal(barrier, inc=1, device_id={"stn": peer}, device_id_type=MESH)
    for peer in seg_peers:
        pl.semaphore_signal(barrier, inc=1, device_id={"seg": peer}, device_id_type=MESH)
    small = []
    for n, (src, dst) in enumerate(
        ((chan_in, chan_ref), (taps_in, taps_ref), (pos_in, pos_ref), (dirs_in, dirs_ref))
    ):
        fetch = pltpu.make_async_copy(src, dst, asem.at[n])
        fetch.start()
        small.append(fetch)
    pending = {}
    for start, wide in ORDER:
        for n in range((start + wide) // PIECE - 1, max(start - PAD, 0) // PIECE - 1, -1):
            if n not in pending:
                fetch = pltpu.make_async_copy(
                    v_ref.at[:, :, pl.ds(n * PIECE, PIECE)],
                    vbuf.at[:, :, pl.ds(PAD + n * PIECE, PIECE)],
                    vsem.at[n],
                )
                fetch.start()
                pending[n] = fetch

    for fetch in small:
        fetch.wait()
    row = lax.broadcasted_iota(jnp.int32, (frame, TAPS * frame), 0)
    lane = lax.broadcasted_iota(jnp.int32, (frame, TAPS * frame), 1)
    channel_of = jnp.zeros((frame, TAPS * frame), jnp.int32)
    for j in range(C):
        channel_of = jnp.where(row // 2 == j, chan_ref[j], channel_of)
    phase_index = jnp.bitwise_and(channel_of * jnp.bitwise_and(lane, frame - 1), frame - 1)
    angles = phase_index.astype(jnp.float32) * (full_turn / frame)
    table = jnp.where(row % 2 == 0, jnp.cos(angles), -jnp.sin(angles))
    taps = jnp.concatenate([taps_ref[m : m + 1, :] for m in range(TAPS)], axis=1)
    mixed = table * taps
    high = mixed.astype(jnp.bfloat16)
    low = (mixed - high.astype(jnp.float32)).astype(jnp.bfloat16)
    mixed = jnp.concatenate([high, low], axis=0)

    def channelize_chunk(c):
        start, wide = ORDER[c]
        for n in sorted(pending):
            if n * PIECE < start + wide and (n + 1) * PIECE > start - PAD:
                pending.pop(n).wait()

        def station(s, carry):
            x = vbuf[s, :, pl.ds(start, wide + PAD)]
            for q in range(0, wide, PIECE):
                width = min(PIECE, wide)
                moved = [x[:, PAD - m + q : PAD - m + q + width] for m in range(TAPS)]
                res = jnp.dot(
                    mixed, jnp.concatenate(moved, axis=0), preferred_element_type=jnp.float32
                )
                res = res[:frame] + res[frame:]
                for t in range(width // PAD):
                    spread[q // PAD + t, pl.ds(pl.multiple_of(s * frame, frame), frame), :] = res[
                        :, t * PAD : (t + 1) * PAD
                    ]
            return carry

        lax.fori_loop(0, local, station, 0, unroll=2)
        for q in range(wide // PAD):
            for j in range(C):
                for a in range(2):
                    picked = spread[q, pl.ds(2 * j + a, local, stride=frame), :]
                    specs[c][j, a, :, q * PAD : (q + 1) * PAD] = picked.astype(jnp.bfloat16)

    def send_chunk(c):
        copies = []
        for d, peer in enumerate(stn_peers):
            copy = pltpu.make_async_remote_copy(
                src_ref=specs[c].at[peer],
                dst_ref=held[c].at[stn],
                send_sem=send_x.at[c, d],
                recv_sem=recv_x.at[c, d],
                device_id={"stn": peer},
                device_id_type=MESH,
            )
            copy.start()
            copies.append(copy)
        held[c][stn] = specs[c][stn]
        return copies

    channelize_chunk(0)
    pl.semaphore_wait(barrier, STN - 1 + SEG - 1)
    halo = pltpu.make_async_remote_copy(
        src_ref=v_ref.at[:, :, pl.ds(snaps - PAD, PAD)],
        dst_ref=vbuf.at[:, :, pl.ds(0, PAD)],
        send_sem=hsem.at[0],
        recv_sem=hsem.at[1],
        device_id={"seg": lax.rem(seg + 1, SEG)},
        device_id_type=MESH,
    )
    halo.start()
    sent = [send_chunk(0)]
    for c in range(1, len(ORDER)):
        if ORDER[c][0] == 0:
            halo.wait()

            @pl.when(seg == 0)
            def _():
                vbuf[:, :, 0:PAD] = jnp.zeros((local, frame, PAD), jnp.bfloat16)

        channelize_chunk(c)
        sent.append(send_chunk(c))

    bearing = dirs_ref[...].astype(jnp.float32) * (full_turn / DIRS)
    frequency = 1.0 + chan_ref[stn].astype(jnp.float32) / C
    east = jnp.broadcast_to(pos_ref[0:1, :], (S, S)).T
    north = jnp.broadcast_to(pos_ref[1:2, :], (S, S)).T
    phases = (full_turn * frequency) * (east * jnp.cos(bearing) + north * jnp.sin(bearing))
    steer_ref[0:S, :] = jnp.cos(phases)
    steer_ref[S : 2 * S, :] = jnp.sin(phases)

    for n, copies in enumerate(sent):
        for copy in copies:
            copy.wait_recv()
        block = stacked(held[n])
        term = lax.dot_general(
            block, block, (((1,), (1,)), ((), ())), preferred_element_type=jnp.float32
        )
        if n == 0:
            gram[...] = term
        else:
            gram[...] += term

    sym = gram[0:S, 0:S] + gram[S : 2 * S, S : 2 * S]
    skew = gram[S : 2 * S, 0:S] - gram[0:S, S : 2 * S]
    row = lax.broadcasted_iota(jnp.int32, (S, S), 0)
    lane = lax.broadcasted_iota(jnp.int32, (S, S), 1)
    part[...] = jnp.where(lane > row, skew, sym).reshape(part.shape)

    across = [lax.rem(seg // SIDE + d, SIDE) * SIDE + lax.rem(seg, SIDE) for d in (2, 1, 3)]
    along = [seg // SIDE * SIDE + lax.rem(seg + d, SIDE) for d in (2, 1, 3)]
    half = SEG // 2

    def exchange(source, target, ways, n):
        copies = []
        for d in range(SIDE - 1):
            for h in range(2):
                copy = pltpu.make_async_remote_copy(
                    src_ref=source.at[pl.ds(h * half, half)],
                    dst_ref=target.at[d, pl.ds(h * half, half)],
                    send_sem=send_a.at[n, d, h],
                    recv_sem=recv_a.at[n, d, h],
                    device_id={"seg": ways[h][d]},
                    device_id_type=MESH,
                )
                copy.start()
                copies.append(copy)
        return copies

    first = exchange(part, landed, (along, across), 0)
    for h in range(2):
        for copy in first[h::2]:
            copy.wait_recv()
        at = pl.ds(h * half, half)
        middle[at] = part[at] + landed[0, at] + landed[1, at] + landed[2, at]
    second = exchange(middle, landed_b, (across, along), 1)
    for h in range(2):
        for copy in second[h::2]:
            copy.wait_recv()
        at = pl.ds(h * half, half)
        packed_ref[at] = middle[at] + landed_b[0, at] + landed_b[1, at] + landed_b[2, at]
    for copies in sent:
        for copy in copies:
            copy.wait_send()
    for copy in first + second:
        copy.wait_send()


def front(voltages, filter_taps, positions, beam_dirs, chan_table):
    local, frame, snaps = voltages.shape
    widths = [wide for _, wide in ORDER]
    rows = S // SEG
    vmem = pl.BlockSpec(memory_space=pltpu.VMEM)
    hbm = pl.BlockSpec(memory_space=pltpu.HBM)
    dma = pltpu.SemaphoreType.DMA
    return pl.pallas_call(
        front_kernel,
        out_shape=(
            jax.ShapeDtypeStruct((SEG, rows, S), jnp.float32),
            jax.ShapeDtypeStruct((2 * S, B), jnp.float32),
            *[jax.ShapeDtypeStruct((STN, 2, local, wide), jnp.bfloat16) for wide in widths],
        ),
        in_specs=[hbm] * 5,
        out_specs=(vmem,) * (2 + len(ORDER)),
        scratch_shapes=[
            *[pltpu.VMEM((STN, 2, local, wide), jnp.bfloat16) for wide in widths],
            pltpu.VMEM(filter_taps.shape, jnp.float32),
            pltpu.VMEM(positions.shape, jnp.float32),
            pltpu.VMEM((1, B), jnp.int32),
            pltpu.SMEM(chan_table.shape, jnp.int32),
            pltpu.VMEM((local, frame, PAD + snaps), jnp.bfloat16),
            pltpu.VMEM((max(widths) // PAD, local * frame, PAD), jnp.float32),
            pltpu.VMEM((2 * S, 2 * S), jnp.float32),
            pltpu.VMEM((SEG, rows, S), jnp.float32),
            pltpu.VMEM((SIDE - 1, SEG, rows, S), jnp.float32),
            pltpu.VMEM((SEG, rows, S), jnp.float32),
            pltpu.VMEM((SIDE - 1, SEG, rows, S), jnp.float32),
            dma((4,)),
            dma((snaps // PIECE,)),
            dma((2,)),
            dma((len(ORDER), STN - 1)),
            dma((len(ORDER), STN - 1)),
            dma((2, SIDE - 1, 2)),
            dma((2, SIDE - 1, 2)),
        ],
        compiler_params=pltpu.CompilerParams(
            collective_id=1, has_side_effects=True, vmem_limit_bytes=48_000_000
        ),
        name="front",
    )(voltages, filter_taps, positions, beam_dirs, chan_table)


def on_device(voltages, filter_taps, positions, beam_dirs, chan_table):
    snap_count = voltages.shape[2]
    stay = lambda x: pltpu.with_memory_space_constraint(x, pltpu.HBM)
    packed, steer, *held = front(stay(voltages), stay(filter_taps), stay(positions), stay(beam_dirs.reshape(1, B)), stay(chan_table))
    beam_out = beams(packed, steer, held, snap_count)
    return beam_out.reshape(1, 2, B, snap_count)


def solution(mesh):
    return jax.shard_map(
        on_device,
        mesh=mesh,
        in_specs=(P("stn", None, "seg"), P(), P(), P(), P()),
        out_specs=P("stn", None, None, "seg"),
        check_vma=False,
    )
```
